512 devices in a mesh: req: 64 (over x, z), head: 8 (over y, core).
Axes of the slice: x: 4, y: 4, z: 16, core: 2. Of those that a mesh axis runs over, the one named last changes fastest.
Arguments:
- tokens: bfloat16 [320, 1024], P('req'), may hold values from -6 to 6
- norm_gain: float32 [1024], replicated, may hold values from 0.1 to 1.9
- w_qkv: bfloat16 [1024, 8, 384], P(None, 'head'), may hold values from -0.1875 to 0.1875
- persist_kv: bfloat16 [8, 16, 256], P('head'), may hold values from -9 to 9
- memory: bfloat16 [64, 8, 128, 128], P('req', 'head'), may hold values from -0.5 to 0.5
- cache_kv: bfloat16 [512, 512, 8, 256], P('req', None, 'head')
- piece_owner: int32 [512], P('req'), may hold values from 0 to 63, as said below
- piece_len: int32 [512], P('req'), may hold values from 1 to 512, as said below
- w_out: bfloat16 [8, 128, 1024], P('head'), may hold values from -0.1875 to 0.1875
Outputs:
- layer_out: bfloat16 [320, 1024], P('req', 'head')
The draws below stay inside these ranges and needn't reach their ends.
Inputs may be any that keep to these rules, and one draw needn't show every extreme that they name: `piece_owner`: every request owns 1 to 16 pieces, and one request owns exactly 16. `piece_len`: some piece is full.
All inputs are finite; a program needn't handle non-finite values.
Results may differ from the reference program's by a relative error of at most 0.009.
The reference program's roundings to bfloat16 on the way (of `normed`, `query` and `head_out`) count: a program that leaves them out, or rounds other values in their place, can miss the bound.
Values may be sent and summed in bfloat16 or wider, within the bound.
No kernel may reach another device: no remote copies, remote signals or barrier semaphores. Data moves between devices by JAX's collectives and lax.ppermute only.
A program may use at most 64 MiB of HBM per device.

```python
import jax
import jax.numpy as jnp
from jax import lax

D = 1024
H = 8
DH = 128
NP = 16
Q = 5
PIECE = 512
MAX_PIECES = 16
REQ_DEV = 1
PIECES_DEV = 8
REQS = 64
SLOTS = 512


def draw_cache_kv(key, part):
    first = jax.random.fold_in(jax.random.fold_in(key, 5), 0)
    shape = (SLOTS, PIECE, H, 2 * DH)
    base = jax.random.normal(first, shape, jnp.float32)
    keys = 2.0 * base[..., :DH]
    values = base[..., DH:]
    return jnp.concatenate([keys, values], axis=-1).astype(jnp.bfloat16)


def draw_piece_owner(key, part):
    first, second, third = jax.random.split(jax.random.fold_in(key, 11), 3)
    spare = PIECES_DEV - REQ_DEV
    devices = SLOTS // PIECES_DEV
    extra = devices * spare
    requests = jnp.arange(REQS, dtype=jnp.int32)
    home_slot = requests // REQ_DEV * PIECES_DEV + requests % REQ_DEV
    spots = jnp.arange(extra, dtype=jnp.int32)
    extra_slot = spots // spare * PIECES_DEV + REQ_DEV + spots % spare
    longest = jax.random.randint(first, (), 0, REQS).astype(jnp.int32)
    others = (longest + 1 + jax.random.permutation(second, REQS - 1).astype(jnp.int32)) % REQS
    later = jnp.maximum(spots - (MAX_PIECES - 1), 0) % (REQS - 1)
    extra_owner = jnp.where(spots < MAX_PIECES - 1, longest, others[later])
    placed = jax.random.permutation(third, extra).astype(jnp.int32)
    owner = jnp.zeros((SLOTS,), jnp.int32).at[home_slot].set(requests)
    owner = owner.at[extra_slot[placed]].set(extra_owner)
    return owner


def draw_piece_len(key, part):
    first, second = jax.random.split(jax.random.fold_in(key, 23), 2)
    lengths = jax.random.randint(first, (SLOTS,), 1, PIECE + 1).astype(jnp.int32)
    where_full = jax.random.randint(second, (), 0, SLOTS)
    return lengths.at[where_full].set(PIECE)


def block_levels(own_key, dims, cuts, low, top_value):
    def one(position, parts):
        heights = jax.random.uniform(jax.random.fold_in(jax.random.fold_in(own_key, 6), position), (parts,), jnp.float32, low / len(cuts), top_value / len(cuts))
        return jnp.repeat(jnp.exp(heights), dims[position] // parts).reshape((-1,) + (1,) * (len(dims) - position - 1))

    factor_of = one(*cuts[0])
    for cut in cuts[1:]:
        factor_of = factor_of * one(*cut)
    return factor_of


def gaussian(stream_key, shape, deviation, bound, cuts=(), kind=jnp.bfloat16):
    gain = block_levels(stream_key, shape, cuts, -0.22, 0.18) if cuts else 1.0
    result = jax.random.normal(stream_key, shape, jnp.float32) * deviation * gain
    return jnp.minimum(jnp.maximum(result, -bound), bound).astype(kind)


def setup_inputs(seed: int = 0) -> dict:
    key_of = jax.random.split(jax.random.key(seed), 10)
    tokens = gaussian(key_of[0], (REQS * Q, D), 1.0, 6.0, ((0, 64),))
    norm_gain = jnp.clip(1.0 + 0.18 * jax.random.normal(key_of[1], (D,), jnp.float32), 0.1, 1.9)
    w_qkv = gaussian(key_of[2], (D, H, 3 * DH), D ** -0.5, 0.1875, ((1, 8),))
    persist_kv = gaussian(key_of[3], (H, NP, 2 * DH), 1.5, 9.0, ((0, 8),))
    memory = gaussian(key_of[4], (REQS, H, DH, DH), DH ** -0.5, 0.5, ((0, 64), (1, 8)))
    cache_kv = draw_cache_kv(jax.random.fold_in(key_of[9], 71), 0)
    piece_owner = draw_piece_owner(jax.random.fold_in(key_of[9], 71), 0)
    piece_len = draw_piece_len(jax.random.fold_in(key_of[9], 71), 0)
    w_out = gaussian(key_of[8], (H, DH, D), (H * DH) ** -0.5, 0.1875, ((0, 8),))
    return dict(tokens=tokens, norm_gain=norm_gain, w_qkv=w_qkv, persist_kv=persist_kv, memory=memory, cache_kv=cache_kv, piece_owner=piece_owner, piece_len=piece_len, w_out=w_out)


masked_score = -1e+30
norm_eps = 1e-06

def reference(tokens, norm_gain, w_qkv, persist_kv, memory, cache_kv, piece_owner, piece_len, w_out):
    f32 = jnp.float32
    xf = tokens.astype(f32)
    normed = (xf * lax.rsqrt(lax.optimization_barrier(jnp.mean(xf * xf, axis=-1, keepdims=True)) + norm_eps) * norm_gain).astype(jnp.bfloat16)
    proj = jnp.einsum('td,dhe->the', normed.astype(f32), w_qkv.astype(f32))
    query = (proj[..., :DH] * DH ** (-0.5)).astype(jnp.bfloat16)
    new_key = proj[..., DH:2 * DH].astype(jnp.bfloat16)
    new_value = proj[..., 2 * DH:].astype(jnp.bfloat16)
    query4 = query.reshape(REQS, Q, H, DH)
    key4 = new_key.reshape(REQS, Q, H, DH)
    value4 = new_value.reshape(REQS, Q, H, DH)

    def slot_part(item):
        block, owner, length = item
        query_rows = lax.dynamic_index_in_dim(query4, owner.astype(jnp.int32), 0, keepdims=False).astype(f32)
        keys = block[..., :DH].astype(f32)
        values = block[..., DH:].astype(f32)
        scores = jnp.einsum('qhe,khe->hqk', query_rows, keys)
        valid = jnp.arange(PIECE) < length
        scores = jnp.where(valid, scores, masked_score)
        peak = lax.optimization_barrier(jnp.max(scores, axis=-1))
        weight = jnp.where(valid, jnp.exp(scores - peak[..., None]), 0.0)
        total = lax.optimization_barrier(jnp.sum(weight, axis=-1))
        rounded = lax.optimization_barrier(weight.astype(jnp.bfloat16)).astype(f32)
        summed = jnp.einsum('hqk,khe->hqe', rounded, values)
        return (peak, total, summed)
    peaks, totals, summed = lax.map(slot_part, (cache_kv, piece_owner, piece_len))
    onehot = piece_owner[:, None] == jnp.arange(REQS, dtype=jnp.int32)[None, :]
    peak_req = lax.optimization_barrier(jnp.max(jnp.where(onehot[:, :, None, None], peaks[:, None], masked_score), axis=0))
    factor = jnp.exp(peaks - peak_req[piece_owner])
    total_cache = jax.ops.segment_sum(totals * factor, piece_owner, num_segments=REQS)
    summed_cache = jax.ops.segment_sum(summed * factor[..., None], piece_owner, num_segments=REQS)
    persist_key = persist_kv[..., :DH].astype(f32)
    persist_value = persist_kv[..., DH:].astype(f32)
    score_persist = jnp.einsum('rqhe,hne->rhqn', query4.astype(f32), persist_key)
    score_new = jnp.einsum('rqhe,rkhe->rhqk', query4.astype(f32), key4.astype(f32))
    causal = jnp.arange(Q)[:, None] >= jnp.arange(Q)[None, :]
    score_new = jnp.where(causal, score_new, masked_score)
    score_own = jnp.concatenate([score_persist, score_new], axis=-1)
    peak_own = lax.optimization_barrier(jnp.max(score_own, axis=-1))
    weight_own = jnp.exp(score_own - peak_own[..., None])
    total_own = lax.optimization_barrier(jnp.sum(weight_own, axis=-1))
    rounded_own = lax.optimization_barrier(weight_own.astype(jnp.bfloat16)).astype(f32)
    summed_own = jnp.einsum('rhqn,hne->rhqe', rounded_own[..., :NP], persist_value)
    summed_own = summed_own + jnp.einsum('rhqk,rkhe->rhqe', rounded_own[..., NP:], value4.astype(f32))
    peak_all = jnp.maximum(peak_req, peak_own)
    scale_cache = jnp.exp(peak_req - peak_all)
    scale_own = jnp.exp(peak_own - peak_all)
    total_all = total_cache * scale_cache + total_own * scale_own
    summed_all = summed_cache * scale_cache[..., None] + summed_own * scale_own[..., None]
    attended = summed_all / total_all[..., None]
    recalled = jnp.einsum('rqhe,rhef->rhqf', query4.astype(f32), memory.astype(f32))
    head_out = (attended + recalled).astype(jnp.bfloat16)
    head_out = jnp.transpose(head_out, (0, 2, 1, 3)).reshape(REQS * Q, H, DH)
    layer_out = jnp.einsum('thd,hdf->tf', head_out.astype(f32), w_out.astype(f32))
    return layer_out.astype(jnp.bfloat16)
```

```python
import jax
import jax.numpy as jnp
from jax import lax
from jax.experimental import pallas as pl
from jax.experimental.pallas import tpu as pltpu
from jax.sharding import PartitionSpec as P

DH = 128
NP = 16
Q = 5
ROWS = 8
M_ROW = 5
L_ROW = 6

masked_score = -1e30
norm_eps = 1e-06
f32 = jnp.float32
bf16 = jnp.bfloat16


def iota(shape, axis):
    return lax.broadcasted_iota(jnp.int32, shape, axis)


def dot(a, b):
    return jnp.dot(a, b, preferred_element_type=f32)


def dot_t(a, b):
    return lax.dot_general(a, b, (((1,), (1,)), ((), ())), preferred_element_type=f32)


def to_row(col, eye):
    return jnp.sum(jnp.where(eye, col, 0.0), axis=0, keepdims=True)


def to_col(row, eye):
    return jnp.sum(jnp.where(eye, jnp.broadcast_to(row, eye.shape), 0.0), axis=1, keepdims=True)


def packed(peak, total, summed, eye, row):
    tail = jnp.where(row == M_ROW, to_row(peak, eye), to_row(total, eye))
    return jnp.where(row < Q, summed, tail)


def project(tokens, gain, w_qkv, query_all, query, new_kv, padded):
    xf = tokens[...].astype(f32)
    inverse = lax.rsqrt(jnp.mean(xf * xf, axis=-1, keepdims=True) + norm_eps)
    normed = (xf * inverse * gain[...]).astype(bf16)
    padded[...] = jnp.zeros_like(padded)
    padded[0:Q, :] = dot(normed, w_qkv[...])
    proj = padded[...]
    q = (proj[:, :DH] * DH ** (-0.5)).astype(bf16)
    query[...] = q
    query_all[...] = jnp.broadcast_to(q[None], query_all.shape)
    new_kv[...] = proj[:, DH:].astype(bf16)


def attend(owner, length, query_all, query, new_kv, persist_kv, memory, cache_kv, dense, own, recalled,
           peak_at, total_at, summed_at):
    pieces, slots = cache_kv.shape[0], cache_kv.shape[1]
    tile = (ROWS, DH)
    row, lane = iota(tile, 0), iota(tile, 1)
    eye = row == lane

    empty = jnp.where(row == M_ROW, masked_score, 0.0).astype(f32)
    dense[...] = jnp.broadcast_to(empty[None], dense.shape)
    for s in range(pieces):
        r = owner[s]
        peak_at[r] = jnp.full(tile, masked_score, f32)
        total_at[r] = jnp.zeros(tile, f32)
        summed_at[r] = jnp.zeros(tile, f32)

    slot = iota((ROWS, slots), 1)
    parts = []
    for s in range(pieces):
        valid = slot < length[s]
        score = jnp.where(valid, dot_t(query_all[owner[s]], cache_kv[s, :, :DH]), masked_score)
        peak = jnp.max(score, axis=-1, keepdims=True)
        weight = jnp.where(valid, jnp.exp(score - peak), 0.0)
        total = jnp.sum(weight, axis=-1, keepdims=True)
        parts.append((peak, total, dot(weight.astype(bf16), cache_kv[s, :, DH:])))

    q = query[...]
    score_persist = dot_t(q, persist_kv[:, :DH])
    score_new = dot_t(q, new_kv[:, :DH])
    causal = iota((ROWS, ROWS), 0) >= iota((ROWS, ROWS), 1)
    score_new = jnp.where(causal, score_new, masked_score)
    peak = jnp.maximum(
        jnp.max(score_persist, axis=-1, keepdims=True), jnp.max(score_new, axis=-1, keepdims=True)
    )
    weight_persist = jnp.exp(score_persist - peak)
    weight_new = jnp.exp(score_new - peak)
    total = jnp.sum(weight_persist, axis=-1, keepdims=True) + jnp.sum(weight_new, axis=-1, keepdims=True)
    summed = dot(weight_persist.astype(bf16), persist_kv[:, DH:])
    summed = summed + dot(weight_new.astype(bf16), new_kv[:, DH:])
    own[...] = packed(jnp.broadcast_to(peak, tile), jnp.broadcast_to(total, tile), summed, eye, row)
    recalled[...] = dot(q, memory[...])

    for s in range(pieces):
        r = owner[s]
        peak, total, summed = parts[s]
        before = peak_at[r]
        joint = jnp.maximum(before, peak)
        scale_before = jnp.exp(before - joint)
        scale = jnp.exp(peak - joint)
        peak_at[r] = joint
        total_at[r] = total_at[r] * scale_before + total * scale
        summed_at[r] = summed_at[r] * scale_before + summed * scale
    for s in range(pieces):
        r = owner[s]
        dense[r] = packed(peak_at[r], total_at[r], summed_at[r], eye, row)


def merge(received, own, recalled, w_out, partial_out):
    tile = (ROWS, DH)
    row, lane = iota(tile, 0), iota(tile, 1)
    eye = row == lane
    sources = received.shape[0]
    blocks = [own[...]] + [received[s] for s in range(sources)]
    top = blocks[0]
    for block in blocks[1:]:
        top = jnp.maximum(top, block)
    peak = top[M_ROW : M_ROW + 1]
    summed = jnp.zeros(tile, f32)
    total = jnp.zeros((1, DH), f32)
    for block in blocks:
        scale = jnp.exp(block[M_ROW : M_ROW + 1] - peak)
        total = total + block[L_ROW : L_ROW + 1] * scale
        summed = summed + block * to_col(scale, eye)
    attended = summed / to_col(total, eye)
    head_out = jnp.where(row < Q, attended + recalled[...], 0.0).astype(bf16)
    terms = dot(head_out, w_out[...])
    for h in range(partial_out.shape[0]):
        partial_out[h] = terms[:, h * DH : (h + 1) * DH]


def vmem(n):
    return [pl.BlockSpec(memory_space=pltpu.VMEM)] * n


def smem(n):
    return [pl.BlockSpec(memory_space=pltpu.SMEM)] * n


def shards(tokens, norm_gain, w_qkv, persist_kv, memory, cache_kv, piece_owner, piece_len, w_out):
    total_reqs = lax.axis_size("req")
    heads = lax.axis_size("head")
    d = tokens.shape[1]
    pieces, slots = cache_kv.shape[:2]
    tile = (ROWS, DH)
    dense_shape = (total_reqs,) + tile

    query_all, query, new_kv = pl.pallas_call(
        project,
        out_shape=(
            jax.ShapeDtypeStruct(dense_shape, bf16),
            jax.ShapeDtypeStruct(tile, bf16),
            jax.ShapeDtypeStruct((ROWS, 2 * DH), bf16),
        ),
        in_specs=vmem(3),
        out_specs=tuple(vmem(3)),
        scratch_shapes=[pltpu.VMEM((ROWS, 3 * DH), f32)],
        name="project",
    )(tokens, norm_gain.reshape(1, d), w_qkv.reshape(d, 3 * DH))

    query_all = lax.all_to_all(query_all, "req", 0, 0, tiled=True)

    dense, own, recalled = pl.pallas_call(
        attend,
        out_shape=(
            jax.ShapeDtypeStruct(dense_shape, f32),
            jax.ShapeDtypeStruct(tile, f32),
            jax.ShapeDtypeStruct(tile, f32),
        ),
        in_specs=smem(2) + vmem(6),
        out_specs=tuple(vmem(3)),
        scratch_shapes=[pltpu.VMEM(dense_shape, f32)] * 3,
        name="attend",
    )(
        piece_owner,
        piece_len,
        query_all,
        query,
        new_kv,
        persist_kv.reshape(NP, 2 * DH),
        memory.reshape(DH, DH),
        cache_kv.reshape(pieces, slots, 2 * DH),
    )

    received = lax.all_to_all(dense, "req", 0, 0, tiled=True)

    partial_out = pl.pallas_call(
        merge,
        out_shape=jax.ShapeDtypeStruct((heads,) + tile, f32),
        in_specs=vmem(4),
        out_specs=vmem(1)[0],
        name="merge",
    )(received, own, recalled, w_out.reshape(DH, d))

    terms = lax.all_to_all(partial_out, "head", 0, 0, tiled=True)
    return jnp.sum(terms, axis=0)[:Q].astype(bf16)


def solution(mesh):
    in_specs = (
        P("req", None),
        P(),
        P(None, "head", None),
        P("head", None, None),
        P("req", "head", None, None),
        P("req", None, "head", None),
        P("req"),
        P("req"),
        P("head", None, None),
    )
    out_specs = P("req", "head")
    return jax.shard_map(shards, mesh=mesh, in_specs=in_specs, out_specs=out_specs, check_vma=False)
```

```python
import jax
import jax.numpy as jnp
from jax import lax
from jax.experimental import pallas as pl
from jax.experimental.pallas import tpu as pltpu
from jax.sharding import PartitionSpec as P

DH = 128
NP = 16
Q = 5
ROWS = 8

masked_score = -1e30
norm_eps = 1e-06
kernel_vmem = 8 << 20
f32 = jnp.float32
bf16 = jnp.bfloat16


def iota(shape, axis):
    return lax.broadcasted_iota(jnp.int32, shape, axis)


def dot(a, b):
    return jnp.dot(a, b, preferred_element_type=f32)


def dot_t(a, b):
    return lax.dot_general(a, b, (((1,), (1,)), ((), ())), preferred_element_type=f32)


def stats_row(peak, total, row, lane):
    picked = jnp.where(lane == row, peak, jnp.where(lane == row + ROWS, total, 0.0))
    return jnp.sum(picked, axis=0, keepdims=True)


def to_col(values, row, lane):
    spread = jnp.broadcast_to(values, row.shape)
    return jnp.sum(jnp.where(row == lane, spread, 0.0), axis=1, keepdims=True)


def packed(peak, total, summed, row, lane):
    stats = stats_row(peak, total, row, lane)
    high = stats.astype(bf16).astype(f32)
    rest = stats - high
    middle = rest.astype(bf16).astype(f32)
    low = rest - middle
    tail = jnp.where(row == Q, high, jnp.where(row == Q + 1, middle, low))
    return jnp.where(row < Q, summed, tail).astype(bf16)


def project(tokens, gain, w_qkv, cache_kv, persist_kv, memory, w_out, query_all, query, new_kv,
            cache_here, persist_here, memory_here, w_out_here, padded, sems):
    pairs = ((cache_kv, cache_here), (persist_kv, persist_here), (memory, memory_here), (w_out, w_out_here))
    copies = [pltpu.make_async_copy(a, b, sems.at[i]) for i, (a, b) in enumerate(pairs)]
    for copy in copies:
        copy.start()
    xf = tokens[...].astype(f32)
    inverse = lax.rsqrt(jnp.mean(xf * xf, axis=-1, keepdims=True) + norm_eps)
    normed = (xf * inverse * gain[...]).astype(bf16)
    padded[...] = jnp.zeros_like(padded)
    padded[0:Q, :] = dot(normed, w_qkv[...])
    proj = padded[...]
    q = (proj[:, :DH] * DH ** (-0.5)).astype(bf16)
    query[...] = q
    query_all[...] = jnp.broadcast_to(q[None], query_all.shape)
    new_kv[...] = proj[:, DH:].astype(bf16)
    for copy in copies:
        copy.wait()


def attend(owner, length, query_all, query, new_kv, persist_kv, memory, cache_kv, dense, own, recalled,
           peak_at, total_at, summed_at):
    pieces, slots = cache_kv.shape[0], cache_kv.shape[1]
    tile = (ROWS, DH)
    row, lane = iota(tile, 0), iota(tile, 1)

    empty = jnp.where((row == Q) & (lane < ROWS), masked_score, 0.0).astype(bf16)
    dense[...] = jnp.broadcast_to(empty[None], dense.shape)
    for s in range(pieces):
        r = owner[s]
        peak_at[r] = jnp.full(tile, masked_score, f32)
        total_at[r] = jnp.zeros(tile, f32)
        summed_at[r] = jnp.zeros(tile, f32)

    slot = iota((ROWS, slots), 1)
    parts = []
    for s in range(pieces):
        valid = slot < length[s]
        score = jnp.where(valid, dot_t(query_all[owner[s]], cache_kv[s, :, :DH]), masked_score)
        peak = jnp.max(score, axis=-1, keepdims=True)
        weight = jnp.where(valid, jnp.exp(score - peak), 0.0)
        total = jnp.sum(weight, axis=-1, keepdims=True)
        parts.append((peak, total, dot(weight.astype(bf16), cache_kv[s, :, DH:])))

    q = query[...]
    score_persist = dot_t(q, persist_kv[:, :DH])
    score_new = dot_t(q, new_kv[:, :DH])
    causal = iota((ROWS, ROWS), 0) >= iota((ROWS, ROWS), 1)
    score_new = jnp.where(causal, score_new, masked_score)
    peak = jnp.maximum(
        jnp.max(score_persist, axis=-1, keepdims=True), jnp.max(score_new, axis=-1, keepdims=True)
    )
    weight_persist = jnp.exp(score_persist - peak)
    weight_new = jnp.exp(score_new - peak)
    total = jnp.sum(weight_persist, axis=-1, keepdims=True) + jnp.sum(weight_new, axis=-1, keepdims=True)
    summed = dot(weight_persist.astype(bf16), persist_kv[:, DH:])
    summed = summed + dot(weight_new.astype(bf16), new_kv[:, DH:])
    stats = stats_row(jnp.broadcast_to(peak, tile), jnp.broadcast_to(total, tile), row, lane)
    own[...] = jnp.where(row < Q, summed, jnp.where(row == Q, stats, 0.0))
    recalled[...] = dot(q, memory[...])

    for s in range(pieces):
        r = owner[s]
        peak, total, summed = parts[s]
        before = peak_at[r]
        joint = jnp.maximum(before, peak)
        scale_before = jnp.exp(before - joint)
        scale = jnp.exp(peak - joint)
        peak_at[r] = joint
        total_at[r] = total_at[r] * scale_before + total * scale
        summed_at[r] = summed_at[r] * scale_before + summed * scale
    for s in range(pieces):
        r = owner[s]
        dense[r] = packed(peak_at[r], total_at[r], summed_at[r], row, lane)


def merge(received, own, recalled, w_out, partial_out):
    tile = (ROWS, DH)
    row, lane = iota(tile, 0), iota(tile, 1)
    sources = received.shape[0]
    blocks = [own[...]] + [received[s].astype(f32) for s in range(sources)]
    stats = [jnp.sum(jnp.where(row >= Q, block, 0.0), axis=0, keepdims=True) for block in blocks]
    peak = stats[0]
    for each in stats[1:]:
        peak = jnp.maximum(peak, each)
    summed = jnp.zeros(tile, f32)
    total = jnp.zeros((ROWS, 1), f32)
    for block, each in zip(blocks, stats):
        scale = jnp.exp(each - peak)
        col = to_col(scale, row, lane)
        total = total + col * to_col(each, row, lane - ROWS)
        summed = summed + block * col
    attended = summed / total
    head_out = jnp.where(row < Q, attended + recalled[...], 0.0).astype(bf16)
    terms = dot(head_out, w_out[...])
    for h in range(partial_out.shape[0]):
        partial_out[h] = terms[:, h * DH : (h + 1) * DH]


def held_in(space, *arrays):
    return [pltpu.with_memory_space_constraint(x, space) for x in arrays]


def vmem(n):
    return [pl.BlockSpec(memory_space=pltpu.VMEM)] * n


def smem(n):
    return [pl.BlockSpec(memory_space=pltpu.SMEM)] * n


def shards(tokens, norm_gain, w_qkv, persist_kv, memory, cache_kv, piece_owner, piece_len, w_out):
    total_reqs = lax.axis_size("req")
    heads = lax.axis_size("head")
    d = tokens.shape[1]
    pieces, slots = cache_kv.shape[:2]
    tile = (ROWS, DH)
    dense_shape = (total_reqs,) + tile

    cache_kv = cache_kv.reshape(pieces, slots, 2 * DH)
    persist_kv = persist_kv.reshape(NP, 2 * DH)
    memory = memory.reshape(DH, DH)
    w_out = w_out.reshape(DH, d)
    fetched = (cache_kv, persist_kv, memory, w_out)
    query_all, query, new_kv, *fetched = pl.pallas_call(
        project,
        out_shape=(
            pltpu.VMEM(dense_shape, bf16),
            pltpu.VMEM(tile, bf16),
            pltpu.VMEM((ROWS, 2 * DH), bf16),
            *(pltpu.VMEM(x.shape, x.dtype) for x in fetched),
        ),
        in_specs=vmem(3) + [pl.BlockSpec(memory_space=pl.ANY)] * len(fetched),
        out_specs=tuple(vmem(3 + len(fetched))),
        scratch_shapes=[pltpu.VMEM((ROWS, 3 * DH), f32), pltpu.SemaphoreType.DMA((len(fetched),))],
        compiler_params=pltpu.CompilerParams(vmem_limit_bytes=kernel_vmem),
        name="project",
    )(*held_in(pltpu.HBM, tokens, norm_gain.reshape(1, d), w_qkv.reshape(d, 3 * DH), *fetched))
    cache_kv, persist_kv, memory, w_out = fetched

    query_all = lax.all_to_all(query_all, "req", 0, 0, tiled=True)

    dense, own, recalled = pl.pallas_call(
        attend,
        out_shape=(pltpu.VMEM(dense_shape, bf16), pltpu.VMEM(tile, f32), pltpu.VMEM(tile, f32)),
        in_specs=smem(2) + vmem(6),
        out_specs=tuple(vmem(3)),
        scratch_shapes=[pltpu.VMEM(dense_shape, f32)] * 3,
        compiler_params=pltpu.CompilerParams(vmem_limit_bytes=kernel_vmem),
        name="attend",
    )(*held_in(pltpu.HBM, piece_owner, piece_len), *held_in(pltpu.VMEM, query_all, query, new_kv, persist_kv, memory, cache_kv))

    received = lax.all_to_all(dense, "req", 0, 0, tiled=True)

    partial_out = pl.pallas_call(
        merge,
        out_shape=pltpu.VMEM((heads,) + tile, f32),
        in_specs=vmem(4),
        out_specs=vmem(1)[0],
        compiler_params=pltpu.CompilerParams(vmem_limit_bytes=kernel_vmem),
        name="merge",
    )(*held_in(pltpu.VMEM, received, own, recalled, w_out))

    terms = lax.all_to_all(partial_out, "head", 0, 0, tiled=True)
    return jnp.sum(terms, axis=0)[:Q].astype(bf16)


def solution(mesh):
    in_specs = (
        P("req", None),
        P(),
        P(None, "head", None),
        P("head", None, None),
        P("req", "head", None, None),
        P("req", None, "head", None),
        P("req"),
        P("req"),
        P("head", None, None),
    )
    out_specs = P("req", "head")
    return jax.shard_map(shards, mesh=mesh, in_specs=in_specs, out_specs=out_specs, check_vma=False)
```

```python
import functools

import jax
import jax.numpy as jnp
from jax import lax
from jax.experimental import pallas as pl
from jax.experimental.pallas import tpu as pltpu
from jax.sharding import Mesh
from jax.sharding import PartitionSpec as P

DH = 128
NP = 16
Q = 5
ROWS = 8

masked_score = -1e30
norm_eps = 1e-06
kernel_vmem = 8 << 20
f32 = jnp.float32
bf16 = jnp.bfloat16


def iota(shape, axis):
    return lax.broadcasted_iota(jnp.int32, shape, axis)


def dot(a, b):
    return jnp.dot(a, b, preferred_element_type=f32)


def dot_t(a, b):
    return lax.dot_general(a, b, (((1,), (1,)), ((), ())), preferred_element_type=f32)


def stats_row(peak, total, row, lane):
    picked = jnp.where(lane == row, peak, jnp.where(lane == row + ROWS, total, 0.0))
    return jnp.sum(picked, axis=0, keepdims=True)


def to_col(values, row, lane):
    spread = jnp.broadcast_to(values, row.shape)
    return jnp.sum(jnp.where(row == lane, spread, 0.0), axis=1, keepdims=True)


def packed(peak, total, summed, row, lane):
    stats = stats_row(peak, total, row, lane)
    high = stats.astype(bf16).astype(f32)
    rest = stats - high
    middle = rest.astype(bf16).astype(f32)
    low = rest - middle
    tail = jnp.where(row == Q, high, jnp.where(row == Q + 1, middle, low))
    return jnp.where(row < Q, summed, tail).astype(bf16)


def project(tokens, gain, w_query, query_all, query, normed, padded):
    xf = tokens[...].astype(f32)
    inverse = lax.rsqrt(jnp.mean(xf * xf, axis=-1, keepdims=True) + norm_eps)
    normed[...] = (xf * inverse * gain[...]).astype(bf16)
    padded[...] = jnp.zeros_like(padded)
    padded[0:Q, :] = dot(normed[...], w_query[...])
    q = (padded[...] * DH ** (-0.5)).astype(bf16)
    query[...] = q
    query_all[...] = jnp.broadcast_to(q[None], query_all.shape)


def own_part(rows, columns, normed, query, w_key, w_value, persist_kv, memory, cache_kv, w_out, owner, length,
             own, recalled, cache_here, w_out_here, place, length_here, padded, owner_here, sems):
    pairs = ((owner, owner_here), (length, length_here), (cache_kv, cache_here), (w_out, w_out_here))
    copies = [pltpu.make_async_copy(a, b, sems.at[i]) for i, (a, b) in enumerate(pairs)]
    for copy in copies:
        copy.start()
    tile = (ROWS, DH)
    row, lane = iota(tile, 0), iota(tile, 1)
    padded[...] = jnp.zeros_like(padded)
    padded[0:Q, :DH] = dot(normed[...], w_key[...])
    padded[0:Q, DH:] = dot(normed[...], w_value[...])
    new_kv = padded[...].astype(bf16)
    q = query[...]
    score_persist = dot_t(q, persist_kv[:, :DH])
    score_new = dot_t(q, new_kv[:, :DH])
    causal = iota((ROWS, ROWS), 0) >= iota((ROWS, ROWS), 1)
    score_new = jnp.where(causal, score_new, masked_score)
    peak = jnp.maximum(
        jnp.max(score_persist, axis=-1, keepdims=True), jnp.max(score_new, axis=-1, keepdims=True)
    )
    weight_persist = jnp.exp(score_persist - peak)
    weight_new = jnp.exp(score_new - peak)
    total = jnp.sum(weight_persist, axis=-1, keepdims=True) + jnp.sum(weight_new, axis=-1, keepdims=True)
    summed = dot(weight_persist.astype(bf16), persist_kv[:, DH:])
    summed = summed + dot(weight_new.astype(bf16), new_kv[:, DH:])
    stats = stats_row(jnp.broadcast_to(peak, tile), jnp.broadcast_to(total, tile), row, lane)
    own[...] = jnp.where(row < Q, summed, jnp.where(row == Q, stats, 0.0))
    recalled[...] = dot(q, memory[...])
    for copy in copies:
        copy.wait()
    for s in range(place.shape[0]):
        r = owner_here[s]
        place[s] = lax.rem(r, columns) * rows + lax.div(r, columns)


def attend(place, length, query_all, cache_kv, dense, peak_at, total_at, summed_at):
    pieces, slots = cache_kv.shape[0], cache_kv.shape[1]
    tile = (ROWS, DH)
    row, lane = iota(tile, 0), iota(tile, 1)

    empty = jnp.where((row == Q) & (lane < ROWS), masked_score, 0.0).astype(bf16)
    dense[...] = jnp.broadcast_to(empty[None], dense.shape)
    for s in range(pieces):
        r = place[s]
        peak_at[r] = jnp.full(tile, masked_score, f32)
        total_at[r] = jnp.zeros(tile, f32)
        summed_at[r] = jnp.zeros(tile, f32)

    slot = iota((ROWS, slots), 1)
    parts = []
    for s in range(pieces):
        valid = slot < length[s]
        score = jnp.where(valid, dot_t(query_all[place[s]], cache_kv[s, :, :DH]), masked_score)
        peak = jnp.max(score, axis=-1, keepdims=True)
        weight = jnp.where(valid, jnp.exp(score - peak), 0.0)
        total = jnp.sum(weight, axis=-1, keepdims=True)
        parts.append((peak, total, dot(weight.astype(bf16), cache_kv[s, :, DH:])))

    for s in range(pieces):
        r = place[s]
        peak, total, summed = parts[s]
        before = peak_at[r]
        joint = jnp.maximum(before, peak)
        scale_before = jnp.exp(before - joint)
        scale = jnp.exp(peak - joint)
        peak_at[r] = joint
        total_at[r] = total_at[r] * scale_before + total * scale
        summed_at[r] = summed_at[r] * scale_before + summed * scale
    for s in range(pieces):
        r = place[s]
        dense[r] = packed(peak_at[r], total_at[r], summed_at[r], row, lane)


def merge(received, own, recalled, w_out, partial_out):
    tile = (ROWS, DH)
    row, lane = iota(tile, 0), iota(tile, 1)
    sources = received.shape[0]
    blocks = [own[...]] + [received[s].astype(f32) for s in range(sources)]
    stats = [jnp.sum(jnp.where(row >= Q, block, 0.0), axis=0, keepdims=True) for block in blocks]
    peak = stats[0]
    for each in stats[1:]:
        peak = jnp.maximum(peak, each)
    summed = jnp.zeros(tile, f32)
    total = jnp.zeros((ROWS, 1), f32)
    for block, each in zip(blocks, stats):
        scale = jnp.exp(each - peak)
        col = to_col(scale, row, lane)
        total = total + col * to_col(each, row, lane - ROWS)
        summed = summed + block * col
    attended = summed / total
    head_out = jnp.where(row < Q, attended + recalled[...], 0.0).astype(bf16)
    terms = dot(head_out, w_out[...])
    for h in range(partial_out.shape[0]):
        partial_out[h] = terms[:, h * DH : (h + 1) * DH]


def held_in(space, *arrays):
    return [pltpu.with_memory_space_constraint(x, space) for x in arrays]


def vmem(n):
    return [pl.BlockSpec(memory_space=pltpu.VMEM)] * n


def smem(n):
    return [pl.BlockSpec(memory_space=pltpu.SMEM)] * n


def hbm(n):
    return [pl.BlockSpec(memory_space=pl.ANY)] * n


def column_block(d, j):
    return pl.BlockSpec((d, DH), lambda i: (0, j))


def shards(tokens, norm_gain, w_qkv, persist_kv, memory, cache_kv, piece_owner, piece_len, w_out):
    rows, columns = lax.axis_size("x"), lax.axis_size("z")
    heads = lax.axis_size("head")
    d = tokens.shape[1]
    pieces, slots = cache_kv.shape[:2]
    tile = (ROWS, DH)
    dense_shape = (rows * columns,) + tile
    params = pltpu.CompilerParams(vmem_limit_bytes=kernel_vmem)

    w_qkv, persist_kv, memory, cache_kv, w_out, piece_owner, piece_len = held_in(
        pltpu.HBM,
        w_qkv.reshape(d, 3 * DH),
        persist_kv.reshape(NP, 2 * DH),
        memory.reshape(DH, DH),
        cache_kv.reshape(pieces, slots, 2 * DH),
        w_out.reshape(DH, d),
        piece_owner,
        piece_len,
    )
    query_all, query, normed = pl.pallas_call(
        project,
        grid=(1,),
        out_shape=(pltpu.VMEM(dense_shape, bf16), pltpu.VMEM(tile, bf16), pltpu.VMEM(tokens.shape, bf16)),
        in_specs=vmem(2) + [column_block(d, 0)],
        out_specs=tuple(vmem(3)),
        scratch_shapes=[pltpu.VMEM(tile, f32)],
        compiler_params=params,
        name="project",
    )(*held_in(pltpu.HBM, tokens, norm_gain.reshape(1, d)), w_qkv)

    query_all = lax.all_to_all(query_all, ("z", "x"), 0, 0, tiled=True)

    own, recalled, cache_kv, w_out, place, piece_len = pl.pallas_call(
        functools.partial(own_part, rows, columns),
        grid=(1,),
        out_shape=(
            pltpu.VMEM(tile, f32),
            pltpu.VMEM(tile, f32),
            pltpu.VMEM(cache_kv.shape, bf16),
            pltpu.VMEM(w_out.shape, bf16),
            pltpu.SMEM((pieces,), jnp.int32),
            pltpu.SMEM((pieces,), jnp.int32),
        ),
        in_specs=vmem(2) + [column_block(d, 1), column_block(d, 2)] + vmem(2) + hbm(4),
        out_specs=tuple(vmem(4) + smem(2)),
        scratch_shapes=[
            pltpu.VMEM((ROWS, 2 * DH), f32),
            pltpu.SMEM((pieces,), jnp.int32),
            pltpu.SemaphoreType.DMA((4,)),
        ],
        compiler_params=params,
        name="own_part",
    )(*held_in(pltpu.VMEM, normed, query), w_qkv, w_qkv, persist_kv, memory, cache_kv, w_out, piece_owner, piece_len)

    dense = pl.pallas_call(
        attend,
        out_shape=pltpu.VMEM(dense_shape, bf16),
        in_specs=smem(2) + vmem(2),
        out_specs=vmem(1)[0],
        scratch_shapes=[pltpu.VMEM(dense_shape, f32)] * 3,
        compiler_params=params,
        name="attend",
    )(*held_in(pltpu.SMEM, place, piece_len), *held_in(pltpu.VMEM, query_all, cache_kv))

    received = lax.all_to_all(dense, ("z", "x"), 0, 0, tiled=True)

    partial_out = pl.pallas_call(
        merge,
        out_shape=pltpu.VMEM((heads,) + tile, f32),
        in_specs=vmem(4),
        out_specs=vmem(1)[0],
        compiler_params=params,
        name="merge",
    )(*held_in(pltpu.VMEM, received, own, recalled, w_out))

    terms = lax.all_to_all(partial_out, "head", 0, 0, tiled=True)
    return jnp.sum(terms, axis=0)[:Q].astype(bf16)


def solution(mesh):
    mesh = Mesh(mesh.devices.reshape(4, 16, 8), ("x", "z", "head"))
    req = ("x", "z")
    in_specs = (
        P(req, None),
        P(),
        P(None, "head", None),
        P("head", None, None),
        P(req, "head", None, None),
        P(req, None, "head", None),
        P(req),
        P(req),
        P("head", None, None),
    )
    out_specs = P(req, "head")
    return jax.shard_map(shards, mesh=mesh, in_specs=in_specs, out_specs=out_specs, check_vma=False)
```

```python
import functools

import jax
import jax.numpy as jnp
from jax import lax
from jax.experimental import pallas as pl
from jax.experimental.pallas import tpu as pltpu
from jax.sharding import PartitionSpec as P

DH = 128
NP = 16
Q = 5
ROWS = 8

masked_score = -1e30
norm_eps = 1e-06
kernel_vmem = 8 << 20
f32 = jnp.float32
bf16 = jnp.bfloat16


def iota(shape, axis):
    return lax.broadcasted_iota(jnp.int32, shape, axis)


def dot(a, b):
    return jnp.dot(a, b, preferred_element_type=f32)


def dot_t(a, b):
    return lax.dot_general(a, b, (((1,), (1,)), ((), ())), preferred_element_type=f32)


def stats_row(peak, total, row, lane):
    picked = jnp.where(lane == row, peak, jnp.where(lane == row + ROWS, total, 0.0))
    return jnp.sum(picked, axis=0, keepdims=True)


def to_col(values, row, lane):
    spread = jnp.broadcast_to(values, row.shape)
    return jnp.sum(jnp.where(row == lane, spread, 0.0), axis=1, keepdims=True)


def packed(peak, total, summed, row, lane):
    stats = stats_row(peak, total, row, lane)
    high = stats.astype(bf16).astype(f32)
    rest = stats - high
    middle = rest.astype(bf16).astype(f32)
    low = rest - middle
    tail = jnp.where(row == Q, high, jnp.where(row == Q + 1, middle, low))
    return jnp.where(row < Q, summed, tail).astype(bf16)


def project(tokens, gain, w_query, query_all, query, normed, padded):
    xf = tokens[...].astype(f32)
    inverse = lax.rsqrt(jnp.mean(xf * xf, axis=-1, keepdims=True) + norm_eps)
    normed[...] = (xf * inverse * gain[...]).astype(bf16)
    padded[...] = jnp.zeros_like(padded)
    padded[0:Q, :] = dot(normed[...], w_query[...])
    q = (padded[...] * DH ** (-0.5)).astype(bf16)
    query[...] = q
    query_all[...] = jnp.broadcast_to(q[None], query_all.shape)


def own_part(rows, columns, normed, query, w_key, w_value, persist_kv, memory, cache_kv, w_out, owner, length,
             own, recalled, cache_here, w_out_here, place, length_here, padded, owner_here, sems):
    pairs = ((owner, owner_here), (length, length_here), (cache_kv, cache_here), (w_out, w_out_here))
    copies = [pltpu.make_async_copy(a, b, sems.at[i]) for i, (a, b) in enumerate(pairs)]
    for copy in copies:
        copy.start()
    tile = (ROWS, DH)
    row, lane = iota(tile, 0), iota(tile, 1)
    padded[...] = jnp.zeros_like(padded)
    padded[0:Q, :DH] = dot(normed[...], w_key[...])
    padded[0:Q, DH:] = dot(normed[...], w_value[...])
    new_kv = padded[...].astype(bf16)
    q = query[...]
    score_persist = dot_t(q, persist_kv[:, :DH])
    score_new = dot_t(q, new_kv[:, :DH])
    causal = iota((ROWS, ROWS), 0) >= iota((ROWS, ROWS), 1)
    score_new = jnp.where(causal, score_new, masked_score)
    peak = jnp.maximum(
        jnp.max(score_persist, axis=-1, keepdims=True), jnp.max(score_new, axis=-1, keepdims=True)
    )
    weight_persist = jnp.exp(score_persist - peak)
    weight_new = jnp.exp(score_new - peak)
    total = jnp.sum(weight_persist, axis=-1, keepdims=True) + jnp.sum(weight_new, axis=-1, keepdims=True)
    summed = dot(weight_persist.astype(bf16), persist_kv[:, DH:])
    summed = summed + dot(weight_new.astype(bf16), new_kv[:, DH:])
    stats = stats_row(jnp.broadcast_to(peak, tile), jnp.broadcast_to(total, tile), row, lane)
    own[...] = jnp.where(row < Q, summed, jnp.where(row == Q, stats, 0.0))
    recalled[...] = dot(q, memory[...])
    for copy in copies:
        copy.wait()
    for s in range(place.shape[0]):
        r = owner_here[s]
        x, z = lax.div(r, columns), lax.rem(r, columns)
        place[s] = lax.rem(z + columns // 2, columns) * rows + lax.rem(x + rows // 2, rows)


def attend(place, length, query_all, cache_kv, dense, peak_at, total_at, summed_at):
    pieces, slots = cache_kv.shape[0], cache_kv.shape[1]
    tile = (ROWS, DH)
    row, lane = iota(tile, 0), iota(tile, 1)

    empty = jnp.where((row == Q) & (lane < ROWS), masked_score, 0.0).astype(bf16)
    dense[...] = jnp.broadcast_to(empty[None], dense.shape)
    for s in range(pieces):
        r = place[s]
        peak_at[r] = jnp.full(tile, masked_score, f32)
        total_at[r] = jnp.zeros(tile, f32)
        summed_at[r] = jnp.zeros(tile, f32)

    slot = iota((ROWS, slots), 1)
    parts = []
    for s in range(pieces):
        valid = slot < length[s]
        score = jnp.where(valid, dot_t(query_all[place[s]], cache_kv[s, :, :DH]), masked_score)
        peak = jnp.max(score, axis=-1, keepdims=True)
        weight = jnp.where(valid, jnp.exp(score - peak), 0.0)
        total = jnp.sum(weight, axis=-1, keepdims=True)
        parts.append((peak, total, dot(weight.astype(bf16), cache_kv[s, :, DH:])))

    for s in range(pieces):
        r = place[s]
        peak, total, summed = parts[s]
        before = peak_at[r]
        joint = jnp.maximum(before, peak)
        scale_before = jnp.exp(before - joint)
        scale = jnp.exp(peak - joint)
        peak_at[r] = joint
        total_at[r] = total_at[r] * scale_before + total * scale
        summed_at[r] = summed_at[r] * scale_before + summed * scale
    for s in range(pieces):
        r = place[s]
        dense[r] = packed(peak_at[r], total_at[r], summed_at[r], row, lane)


def merge(received, own, recalled, w_out, partial_out):
    tile = (ROWS, DH)
    row, lane = iota(tile, 0), iota(tile, 1)
    sources = received.shape[0]
    blocks = [own[...]] + [received[s].astype(f32) for s in range(sources)]
    stats = [jnp.sum(jnp.where(row >= Q, block, 0.0), axis=0, keepdims=True) for block in blocks]
    peak = stats[0]
    for each in stats[1:]:
        peak = jnp.maximum(peak, each)
    summed = jnp.zeros(tile, f32)
    total = jnp.zeros((ROWS, 1), f32)
    for block, each in zip(blocks, stats):
        scale = jnp.exp(each - peak)
        col = to_col(scale, row, lane)
        total = total + col * to_col(each, row, lane - ROWS)
        summed = summed + block * col
    attended = summed / total
    head_out = jnp.where(row < Q, attended + recalled[...], 0.0).astype(bf16)
    terms = dot(head_out, w_out[...])
    for h in range(partial_out.shape[0]):
        partial_out[h] = terms[:, h * DH : (h + 1) * DH]


def held_in(space, *arrays):
    return [pltpu.with_memory_space_constraint(x, space) for x in arrays]


def vmem(n):
    return [pl.BlockSpec(memory_space=pltpu.VMEM)] * n


def smem(n):
    return [pl.BlockSpec(memory_space=pltpu.SMEM)] * n


def hbm(n):
    return [pl.BlockSpec(memory_space=pl.ANY)] * n


def column_block(d, j):
    return pl.BlockSpec((d, DH), lambda i: (0, j))


def exchange_order(rows, columns):
    return [
        (x + rows // 2) % rows * columns + (z + columns // 2) % columns for z in range(columns) for x in range(rows)
    ]


def shards(rows, columns, tokens, norm_gain, w_qkv, persist_kv, memory, cache_kv, piece_owner, piece_len, w_out):
    groups = [exchange_order(rows, columns)]
    heads = lax.axis_size("head")
    d = tokens.shape[1]
    pieces, slots = cache_kv.shape[:2]
    tile = (ROWS, DH)
    dense_shape = (rows * columns,) + tile
    params = pltpu.CompilerParams(vmem_limit_bytes=kernel_vmem)

    w_qkv, persist_kv, memory, cache_kv, w_out, piece_owner, piece_len = held_in(
        pltpu.HBM,
        w_qkv.reshape(d, 3 * DH),
        persist_kv.reshape(NP, 2 * DH),
        memory.reshape(DH, DH),
        cache_kv.reshape(pieces, slots, 2 * DH),
        w_out.reshape(DH, d),
        piece_owner,
        piece_len,
    )
    query_all, query, normed = pl.pallas_call(
        project,
        grid=(1,),
        out_shape=(pltpu.VMEM(dense_shape, bf16), pltpu.VMEM(tile, bf16), pltpu.VMEM(tokens.shape, bf16)),
        in_specs=vmem(2) + [column_block(d, 0)],
        out_specs=tuple(vmem(3)),
        scratch_shapes=[pltpu.VMEM(tile, f32)],
        compiler_params=params,
        name="project",
    )(*held_in(pltpu.HBM, tokens, norm_gain.reshape(1, d)), w_qkv)

    query_all = lax.all_to_all(query_all, "req", 0, 0, axis_index_groups=groups, tiled=True)

    own, recalled, cache_kv, w_out, place, piece_len = pl.pallas_call(
        functools.partial(own_part, rows, columns),
        grid=(1,),
        out_shape=(
            pltpu.VMEM(tile, f32),
            pltpu.VMEM(tile, f32),
            pltpu.VMEM(cache_kv.shape, bf16),
            pltpu.VMEM(w_out.shape, bf16),
            pltpu.SMEM((pieces,), jnp.int32),
            pltpu.SMEM((pieces,), jnp.int32),
        ),
        in_specs=vmem(2) + [column_block(d, 1), column_block(d, 2)] + vmem(2) + hbm(4),
        out_specs=tuple(vmem(4) + smem(2)),
        scratch_shapes=[
            pltpu.VMEM((ROWS, 2 * DH), f32),
            pltpu.SMEM((pieces,), jnp.int32),
            pltpu.SemaphoreType.DMA((4,)),
        ],
        compiler_params=params,
        name="own_part",
    )(*held_in(pltpu.VMEM, normed, query), w_qkv, w_qkv, persist_kv, memory, cache_kv, w_out, piece_owner, piece_len)

    dense = pl.pallas_call(
        attend,
        out_shape=pltpu.VMEM(dense_shape, bf16),
        in_specs=smem(2) + vmem(2),
        out_specs=vmem(1)[0],
        scratch_shapes=[pltpu.VMEM(dense_shape, f32)] * 3,
        compiler_params=params,
        name="attend",
    )(*held_in(pltpu.SMEM, place, piece_len), *held_in(pltpu.VMEM, query_all, cache_kv))

    received = lax.all_to_all(dense, "req", 0, 0, axis_index_groups=groups, tiled=True)

    partial_out = pl.pallas_call(
        merge,
        out_shape=pltpu.VMEM((heads,) + tile, f32),
        in_specs=vmem(4),
        out_specs=vmem(1)[0],
        compiler_params=params,
        name="merge",
    )(*held_in(pltpu.VMEM, received, own, recalled, w_out))

    terms = lax.all_to_all(partial_out, "head", 0, 0, tiled=True)
    return jnp.sum(terms, axis=0)[:Q].astype(bf16)


def solution(mesh):
    in_specs = (
        P("req", None),
        P(),
        P(None, "head", None),
        P("head", None, None),
        P("req", "head", None, None),
        P("req", None, "head", None),
        P("req"),
        P("req"),
        P("head", None, None),
    )
    out_specs = P("req", "head")
    step = functools.partial(shards, 4, mesh.shape["req"] // 4)
    return jax.shard_map(step, mesh=mesh, in_specs=in_specs, out_specs=out_specs, check_vma=False)
```

```python
import functools

import jax
import jax.numpy as jnp
from jax import lax
from jax.experimental import pallas as pl
from jax.experimental.pallas import tpu as pltpu
from jax.sharding import PartitionSpec as P

DH = 128
NP = 16
Q = 5
ROWS = 8
PAIRS = 3
STRIDE = 16
PARTS = 3

masked_score = -1e30
norm_eps = 1e-06
kernel_vmem = 8 << 20
f32 = jnp.float32
bf16 = jnp.bfloat16


def iota(shape, axis):
    return lax.broadcasted_iota(jnp.int32, shape, axis)


def dot(a, b):
    return jnp.dot(a, b, preferred_element_type=f32)


def dot_t(a, b):
    return lax.dot_general(a, b, (((1,), (1,)), ((), ())), preferred_element_type=f32)


def stats_at(row, lane, offset):
    return (lane % STRIDE == row + offset) & (lane < PARTS * STRIDE)


def stats_row(peak, total, row, lane):
    picked = jnp.where(stats_at(row, lane, 0), peak, jnp.where(stats_at(row, lane, ROWS), total, 0.0))
    return jnp.sum(picked, axis=0, keepdims=True)


def stats_col(block, row, lane, offset):
    spread = jnp.broadcast_to(block[Q : Q + 1], row.shape)
    return jnp.sum(jnp.where(stats_at(row, lane, offset), spread, 0.0), axis=1, keepdims=True)


def packed(peak, total, summed, row, lane):
    stats = stats_row(peak, total, row, lane)
    high = stats.astype(bf16).astype(f32)
    rest = stats - high
    middle = rest.astype(bf16).astype(f32)
    place = lane[:1]
    tail = jnp.where(place < STRIDE, high, jnp.where(place < 2 * STRIDE, middle, rest - middle))
    return jnp.where(row < Q, summed, tail)


def put_block(target, index, tile):
    for k in range(PAIRS):
        target[index, k] = tile[2 * k : 2 * k + 2].astype(bf16)


def get_block(source, index):
    pairs = [source[index, k].astype(f32) for k in range(PAIRS)]
    return jnp.concatenate(pairs + [jnp.zeros((ROWS - 2 * PAIRS, DH), f32)], axis=0)


def project(tokens, gain, w_query, query_all, query, normed, padded):
    xf = tokens[...].astype(f32)
    inverse = lax.rsqrt(jnp.mean(xf * xf, axis=-1, keepdims=True) + norm_eps)
    normed[...] = (xf * inverse * gain[...]).astype(bf16)
    padded[...] = jnp.zeros_like(padded)
    padded[0:Q, :] = dot(normed[...], w_query[...])
    q = padded[...] * DH ** (-0.5)
    query[...] = q.astype(bf16)
    for k in range(PAIRS):
        pair = q[2 * k : 2 * k + 2].astype(bf16)
        query_all[:, k] = jnp.broadcast_to(pair[None], (query_all.shape[0],) + pair.shape)


def own_part(rows, columns, normed, query, w_key, w_value, persist_kv, memory, cache_kv, w_out, owner, length,
             own, recalled, cache_here, w_out_here, place, length_here, padded, owner_here, sems):
    pairs = ((owner, owner_here), (length, length_here), (cache_kv, cache_here), (w_out, w_out_here))
    copies = [pltpu.make_async_copy(a, b, sems.at[i]) for i, (a, b) in enumerate(pairs)]
    for copy in copies:
        copy.start()
    tile = (ROWS, DH)
    row, lane = iota(tile, 0), iota(tile, 1)
    padded[...] = jnp.zeros_like(padded)
    padded[0:Q, :DH] = dot(normed[...], w_key[...])
    padded[0:Q, DH:] = dot(normed[...], w_value[...])
    new_kv = padded[...].astype(bf16)
    q = query[...]
    score_persist = dot_t(q, persist_kv[:, :DH])
    score_new = dot_t(q, new_kv[:, :DH])
    causal = iota((ROWS, ROWS), 0) >= iota((ROWS, ROWS), 1)
    score_new = jnp.where(causal, score_new, masked_score)
    peak = jnp.maximum(
        jnp.max(score_persist, axis=-1, keepdims=True), jnp.max(score_new, axis=-1, keepdims=True)
    )
    weight_persist = jnp.exp(score_persist - peak)
    weight_new = jnp.exp(score_new - peak)
    total = jnp.sum(weight_persist, axis=-1, keepdims=True) + jnp.sum(weight_new, axis=-1, keepdims=True)
    summed = dot(weight_persist.astype(bf16), persist_kv[:, DH:])
    summed = summed + dot(weight_new.astype(bf16), new_kv[:, DH:])
    stats = stats_row(jnp.broadcast_to(peak, tile), jnp.broadcast_to(total, tile), row, lane)
    own[...] = jnp.where(row < Q, summed, jnp.where((row == Q) & (lane < STRIDE), stats, 0.0))
    recalled[...] = dot(q, memory[...])
    for copy in copies:
        copy.wait()
    for s in range(place.shape[0]):
        r = owner_here[s]
        x, z = lax.div(r, columns), lax.rem(r, columns)
        place[s] = lax.rem(z + columns // 2, columns) * rows + lax.rem(x + rows // 2, rows)


def attend(place, length, query_all, cache_kv, dense):
    pieces, slots = cache_kv.shape[0], cache_kv.shape[1]
    tile = (ROWS, DH)
    row, lane = iota(tile, 0), iota(tile, 1)

    for k in range(PAIRS):
        pair = (2, DH)
        holds_peak = (iota(pair, 0) + 2 * k == Q) & (iota(pair, 1) < ROWS)
        empty = jnp.where(holds_peak, masked_score, 0.0).astype(bf16)
        dense[:, k] = jnp.broadcast_to(empty[None], (dense.shape[0],) + pair)

    slot = iota((ROWS, slots), 1)
    parts = []
    for s in range(pieces):
        valid = slot < length[s]
        score = jnp.where(valid, dot_t(get_block(query_all, place[s]).astype(bf16), cache_kv[s, :, :DH]), masked_score)
        peak = jnp.max(score, axis=-1, keepdims=True)
        weight = jnp.where(valid, jnp.exp(score - peak), 0.0)
        total = jnp.sum(weight, axis=-1, keepdims=True)
        summed = dot(weight.astype(bf16), cache_kv[s, :, DH:])
        parts.append((jnp.broadcast_to(peak, tile), jnp.broadcast_to(total, tile), summed))

    for s in range(pieces):
        r = place[s]
        peaks = [jnp.where(jnp.full(tile, place[t], jnp.int32) == r, parts[t][0], 2 * masked_score) for t in range(pieces)]
        top = functools.reduce(jnp.maximum, peaks)
        scales = [jnp.exp(peak - top) for peak in peaks]
        total = sum(scale * part[1] for scale, part in zip(scales, parts))
        summed = sum(scale * part[2] for scale, part in zip(scales, parts))
        put_block(dense, r, packed(top, total, summed, row, lane))


def merge(received, own, recalled, w_out, partial_out):
    tile = (ROWS, DH)
    row, lane = iota(tile, 0), iota(tile, 1)
    sources = received.shape[0]
    blocks = [own[...]] + [get_block(received, s) for s in range(sources)]
    peaks = [stats_col(block, row, lane, 0) for block in blocks]
    peak = functools.reduce(jnp.maximum, peaks)
    summed = jnp.zeros(tile, f32)
    total = jnp.zeros((ROWS, 1), f32)
    for block, each in zip(blocks, peaks):
        scale = jnp.exp(each - peak)
        total = total + scale * stats_col(block, row, lane, ROWS)
        summed = summed + scale * block
    attended = summed / total
    head_out = jnp.where(row < Q, attended + recalled[...], 0.0).astype(bf16)
    terms = dot(head_out, w_out[...])
    for h in range(partial_out.shape[0]):
        to = (h + partial_out.shape[0] // 2) % partial_out.shape[0]
        partial_out[h] = terms[:, to * DH : (to + 1) * DH]


def held_in(space, *arrays):
    return [pltpu.with_memory_space_constraint(x, space) for x in arrays]


def vmem(n):
    return [pl.BlockSpec(memory_space=pltpu.VMEM)] * n


def smem(n):
    return [pl.BlockSpec(memory_space=pltpu.SMEM)] * n


def hbm(n):
    return [pl.BlockSpec(memory_space=pl.ANY)] * n


def column_block(d, j):
    return pl.BlockSpec((d, DH), lambda i: (0, j))


def exchange_order(rows, columns):
    return [
        (x + rows // 2) % rows * columns + (z + columns // 2) % columns for z in range(columns) for x in range(rows)
    ]


def shards(rows, columns, tokens, norm_gain, w_qkv, persist_kv, memory, cache_kv, piece_owner, piece_len, w_out):
    groups = [exchange_order(rows, columns)]
    heads = lax.axis_size("head")
    d = tokens.shape[1]
    pieces, slots = cache_kv.shape[:2]
    tile = (ROWS, DH)
    dense_shape = (rows * columns, PAIRS, 2, DH)
    params = pltpu.CompilerParams(vmem_limit_bytes=kernel_vmem)

    w_qkv, persist_kv, memory, cache_kv, w_out, piece_owner, piece_len = held_in(
        pltpu.HBM,
        w_qkv.reshape(d, 3 * DH),
        persist_kv.reshape(NP, 2 * DH),
        memory.reshape(DH, DH),
        cache_kv.reshape(pieces, slots, 2 * DH),
        w_out.reshape(DH, d),
        piece_owner,
        piece_len,
    )
    query_all, query, normed = pl.pallas_call(
        project,
        grid=(1,),
        out_shape=(pltpu.VMEM(dense_shape, bf16), pltpu.VMEM(tile, bf16), pltpu.VMEM(tokens.shape, bf16)),
        in_specs=vmem(2) + [column_block(d, 0)],
        out_specs=tuple(vmem(3)),
        scratch_shapes=[pltpu.VMEM(tile, f32)],
        compiler_params=params,
        name="project",
    )(*held_in(pltpu.HBM, tokens, norm_gain.reshape(1, d)), w_qkv)

    query_all = lax.all_to_all(query_all, "req", 0, 0, axis_index_groups=groups, tiled=True)

    own, recalled, cache_kv, w_out, place, piece_len = pl.pallas_call(
        functools.partial(own_part, rows, columns),
        grid=(1,),
        out_shape=(
            pltpu.VMEM(tile, f32),
            pltpu.VMEM(tile, f32),
            pltpu.VMEM(cache_kv.shape, bf16),
            pltpu.VMEM(w_out.shape, bf16),
            pltpu.SMEM((pieces,), jnp.int32),
            pltpu.SMEM((pieces,), jnp.int32),
        ),
        in_specs=vmem(2) + [column_block(d, 1), column_block(d, 2)] + vmem(2) + hbm(4),
        out_specs=tuple(vmem(4) + smem(2)),
        scratch_shapes=[
            pltpu.VMEM((ROWS, 2 * DH), f32),
            pltpu.SMEM((pieces,), jnp.int32),
            pltpu.SemaphoreType.DMA((4,)),
        ],
        compiler_params=params,
        name="own_part",
    )(*held_in(pltpu.VMEM, normed, query), w_qkv, w_qkv, persist_kv, memory, cache_kv, w_out, piece_owner, piece_len)

    dense = pl.pallas_call(
        attend,
        out_shape=pltpu.VMEM(dense_shape, bf16),
        in_specs=smem(2) + vmem(2),
        out_specs=vmem(1)[0],
        compiler_params=params,
        name="attend",
    )(*held_in(pltpu.SMEM, place, piece_len), *held_in(pltpu.VMEM, query_all, cache_kv))

    received = lax.all_to_all(dense, "req", 0, 0, axis_index_groups=groups, tiled=True)

    partial_out = pl.pallas_call(
        merge,
        out_shape=pltpu.VMEM((heads,) + tile, f32),
        in_specs=vmem(4),
        out_specs=vmem(1)[0],
        compiler_params=params,
        name="merge",
    )(*held_in(pltpu.VMEM, received, own, recalled, w_out))

    half = heads // 2
    head_groups = [[(h + half) % heads for h in range(heads)]]
    terms = lax.all_to_all(partial_out, "head", 0, 0, axis_index_groups=head_groups, tiled=True)
    return jnp.sum(terms, axis=0)[:Q].astype(bf16)


def solution(mesh):
    in_specs = (
        P("req", None),
        P(),
        P(None, "head", None),
        P("head", None, None),
        P("req", "head", None, None),
        P("req", None, "head", None),
        P("req"),
        P("req"),
        P("head", None, None),
    )
    out_specs = P("req", "head")
    step = functools.partial(shards, 4, mesh.shape["req"] // 4)
    return jax.shard_map(step, mesh=mesh, in_specs=in_specs, out_specs=out_specs, check_vma=False)
```

```python
import functools

import jax
import jax.numpy as jnp
from jax import lax
from jax.experimental import pallas as pl
from jax.experimental.pallas import tpu as pltpu
from jax.sharding import PartitionSpec as P

DH = 128
NP = 16
Q = 5
ROWS = 8
PAIRS = 3
STRIDE = 16
PARTS = 3

masked_score = -1e30
norm_eps = 1e-06
kernel_vmem = 8 << 20
f32 = jnp.float32
bf16 = jnp.bfloat16


def iota(shape, axis):
    return lax.broadcasted_iota(jnp.int32, shape, axis)


def dot(a, b):
    return jnp.dot(a, b, preferred_element_type=f32)


def dot_t(a, b):
    return lax.dot_general(a, b, (((1,), (1,)), ((), ())), preferred_element_type=f32)


def stats_at(row, lane, offset):
    return (lane % STRIDE == row + offset) & (lane < PARTS * STRIDE)


def stats_row(peak, total, row, lane):
    picked = jnp.where(stats_at(row, lane, 0), peak, jnp.where(stats_at(row, lane, ROWS), total, 0.0))
    return jnp.sum(picked, axis=0, keepdims=True)


def stats_col(block, row, lane, offset):
    spread = jnp.broadcast_to(block[Q : Q + 1], row.shape)
    return jnp.sum(jnp.where(stats_at(row, lane, offset), spread, 0.0), axis=1, keepdims=True)


def packed(peak, total, summed, row, lane):
    stats = stats_row(peak, total, row, lane)
    high = stats.astype(bf16).astype(f32)
    rest = stats - high
    middle = rest.astype(bf16).astype(f32)
    place = lane[:1]
    tail = jnp.where(place < STRIDE, high, jnp.where(place < 2 * STRIDE, middle, rest - middle))
    return jnp.where(row < Q, summed, tail)


def put_block(target, index, tile):
    for k in range(PAIRS):
        target[index, k] = tile[2 * k : 2 * k + 2].astype(bf16)


def get_block(source, index):
    pairs = [source[index, k].astype(f32) for k in range(PAIRS)]
    return jnp.concatenate(pairs + [jnp.zeros((ROWS - 2 * PAIRS, DH), f32)], axis=0)


def project(tokens, gain, w_query, query_all, query, normed, padded):
    xf = tokens[...].astype(f32)
    inverse = lax.rsqrt(jnp.mean(xf * xf, axis=-1, keepdims=True) + norm_eps)
    normed[...] = (xf * inverse * gain[...]).astype(bf16)
    padded[...] = jnp.zeros_like(padded)
    padded[0:Q, :] = dot(normed[...], w_query[...])
    q = padded[...] * DH ** (-0.5)
    query[...] = q.astype(bf16)
    for k in range(PAIRS):
        pair = q[2 * k : 2 * k + 2].astype(bf16)
        query_all[:, k] = jnp.broadcast_to(pair[None], (query_all.shape[0],) + pair.shape)


def own_part(rows, columns, normed, query, w_key, w_value, persist_kv, memory, cache_kv, w_out, owner, length,
             own, recalled, cache_here, w_out_here, place, length_here, padded, owner_here, sems):
    pairs = ((owner, owner_here), (length, length_here), (cache_kv, cache_here), (w_out, w_out_here))
    copies = [pltpu.make_async_copy(a, b, sems.at[i]) for i, (a, b) in enumerate(pairs)]
    for copy in copies:
        copy.start()
    tile = (ROWS, DH)
    row, lane = iota(tile, 0), iota(tile, 1)
    padded[...] = jnp.zeros_like(padded)
    padded[0:Q, :DH] = dot(normed[...], w_key[...])
    padded[0:Q, DH:] = dot(normed[...], w_value[...])
    new_kv = padded[...].astype(bf16)
    q = query[...]
    score_persist = dot_t(q, persist_kv[:, :DH])
    score_new = dot_t(q, new_kv[:, :DH])
    causal = iota((ROWS, ROWS), 0) >= iota((ROWS, ROWS), 1)
    score_new = jnp.where(causal, score_new, masked_score)
    peak = jnp.maximum(
        jnp.max(score_persist, axis=-1, keepdims=True), jnp.max(score_new, axis=-1, keepdims=True)
    )
    weight_persist = jnp.exp(score_persist - peak)
    weight_new = jnp.exp(score_new - peak)
    total = jnp.sum(weight_persist, axis=-1, keepdims=True) + jnp.sum(weight_new, axis=-1, keepdims=True)
    summed = dot(weight_persist.astype(bf16), persist_kv[:, DH:])
    summed = summed + dot(weight_new.astype(bf16), new_kv[:, DH:])
    stats = stats_row(jnp.broadcast_to(peak, tile), jnp.broadcast_to(total, tile), row, lane)
    own[...] = jnp.where(row < Q, summed, jnp.where((row == Q) & (lane < STRIDE), stats, 0.0))
    recalled[...] = dot(q, memory[...])
    for copy in copies:
        copy.wait()
    for s in range(place.shape[0]):
        r = owner_here[s]
        x, z = lax.div(r, columns), lax.rem(r, columns)
        place[s] = lax.rem(z + columns // 2, columns) * rows + lax.rem(x + rows // 2, rows)


def attend(place, length, query_all, cache_kv, dense):
    pieces, slots = cache_kv.shape[0], cache_kv.shape[1]
    tile = (ROWS, DH)
    row, lane = iota(tile, 0), iota(tile, 1)

    for k in range(PAIRS):
        pair = (2, DH)
        holds_peak = (iota(pair, 0) + 2 * k == Q) & (iota(pair, 1) < ROWS)
        empty = jnp.where(holds_peak, masked_score, 0.0).astype(bf16)
        dense[:, k] = jnp.broadcast_to(empty[None], (dense.shape[0],) + pair)

    slot = iota((ROWS, slots), 1)
    scores = [
        dot_t(get_block(query_all, place[s]).astype(bf16), cache_kv[s, :, :DH]) for s in range(pieces)
    ]
    weights, peaks, totals = [], [], []
    for s in range(pieces):
        valid = slot < length[s]
        score = jnp.where(valid, scores[s], masked_score)
        peak = jnp.max(score, axis=-1, keepdims=True)
        weight = jnp.where(valid, jnp.exp(score - peak), 0.0)
        weights.append(weight.astype(bf16))
        peaks.append(jnp.broadcast_to(peak, tile))
        totals.append(jnp.broadcast_to(jnp.sum(weight, axis=-1, keepdims=True), tile))
    summeds = [dot(weights[s], cache_kv[s, :, DH:]) for s in range(pieces)]
    parts = list(zip(peaks, totals, summeds))

    for s in range(pieces):
        r = place[s]
        peaks = [jnp.where(jnp.full(tile, place[t], jnp.int32) == r, parts[t][0], 2 * masked_score) for t in range(pieces)]
        top = functools.reduce(jnp.maximum, peaks)
        scales = [jnp.exp(peak - top) for peak in peaks]
        total = sum(scale * part[1] for scale, part in zip(scales, parts))
        summed = sum(scale * part[2] for scale, part in zip(scales, parts))
        put_block(dense, r, packed(top, total, summed, row, lane))


def merge(received, own, recalled, w_out, partial_out):
    tile = (ROWS, DH)
    row, lane = iota(tile, 0), iota(tile, 1)
    sources = received.shape[0]
    blocks = [own[...]] + [get_block(received, s) for s in range(sources)]
    peaks = [stats_col(block, row, lane, 0) for block in blocks]
    peak = functools.reduce(jnp.maximum, peaks)
    summed = jnp.zeros(tile, f32)
    total = jnp.zeros((ROWS, 1), f32)
    for block, each in zip(blocks, peaks):
        scale = jnp.exp(each - peak)
        total = total + scale * stats_col(block, row, lane, ROWS)
        summed = summed + scale * block
    attended = summed / total
    head_out = jnp.where(row < Q, attended + recalled[...], 0.0).astype(bf16)
    terms = dot(head_out, w_out[...])
    for h in range(partial_out.shape[0]):
        to = (h + partial_out.shape[0] // 2) % partial_out.shape[0]
        partial_out[h] = terms[:, to * DH : (to + 1) * DH]


def held_in(space, *arrays):
    return [pltpu.with_memory_space_constraint(x, space) for x in arrays]


def vmem(n):
    return [pl.BlockSpec(memory_space=pltpu.VMEM)] * n


def smem(n):
    return [pl.BlockSpec(memory_space=pltpu.SMEM)] * n


def hbm(n):
    return [pl.BlockSpec(memory_space=pl.ANY)] * n


def column_block(d, j):
    return pl.BlockSpec((d, DH), lambda i: (0, j))


def exchange_order(rows, columns):
    return [
        (x + rows // 2) % rows * columns + (z + columns // 2) % columns for z in range(columns) for x in range(rows)
    ]


def shards(rows, columns, tokens, norm_gain, w_qkv, persist_kv, memory, cache_kv, piece_owner, piece_len, w_out):
    groups = [exchange_order(rows, columns)]
    heads = lax.axis_size("head")
    d = tokens.shape[1]
    pieces, slots = cache_kv.shape[:2]
    tile = (ROWS, DH)
    dense_shape = (rows * columns, PAIRS, 2, DH)
    params = pltpu.CompilerParams(vmem_limit_bytes=kernel_vmem)

    w_qkv, persist_kv, memory, cache_kv, w_out, piece_owner, piece_len = held_in(
        pltpu.HBM,
        w_qkv.reshape(d, 3 * DH),
        persist_kv.reshape(NP, 2 * DH),
        memory.reshape(DH, DH),
        cache_kv.reshape(pieces, slots, 2 * DH),
        w_out.reshape(DH, d),
        piece_owner,
        piece_len,
    )
    query_all, query, normed = pl.pallas_call(
        project,
        grid=(1,),
        out_shape=(pltpu.VMEM(dense_shape, bf16), pltpu.VMEM(tile, bf16), pltpu.VMEM(tokens.shape, bf16)),
        in_specs=vmem(2) + [column_block(d, 0)],
        out_specs=tuple(vmem(3)),
        scratch_shapes=[pltpu.VMEM(tile, f32)],
        compiler_params=params,
        name="project",
    )(*held_in(pltpu.HBM, tokens, norm_gain.reshape(1, d)), w_qkv)

    query_all = lax.all_to_all(query_all, "req", 0, 0, axis_index_groups=groups, tiled=True)

    own, recalled, cache_kv, w_out, place, piece_len = pl.pallas_call(
        functools.partial(own_part, rows, columns),
        grid=(1,),
        out_shape=(
            pltpu.VMEM(tile, f32),
            pltpu.VMEM(tile, f32),
            pltpu.VMEM(cache_kv.shape, bf16),
            pltpu.VMEM(w_out.shape, bf16),
            pltpu.SMEM((pieces,), jnp.int32),
            pltpu.SMEM((pieces,), jnp.int32),
        ),
        in_specs=vmem(2) + [column_block(d, 1), column_block(d, 2)] + vmem(2) + hbm(4),
        out_specs=tuple(vmem(4) + smem(2)),
        scratch_shapes=[
            pltpu.VMEM((ROWS, 2 * DH), f32),
            pltpu.SMEM((pieces,), jnp.int32),
            pltpu.SemaphoreType.DMA((4,)),
        ],
        compiler_params=params,
        name="own_part",
    )(*held_in(pltpu.VMEM, normed, query), w_qkv, w_qkv, persist_kv, memory, cache_kv, w_out, piece_owner, piece_len)

    dense = pl.pallas_call(
        attend,
        out_shape=pltpu.VMEM(dense_shape, bf16),
        in_specs=smem(2) + vmem(2),
        out_specs=vmem(1)[0],
        compiler_params=params,
        name="attend",
    )(*held_in(pltpu.SMEM, place, piece_len), *held_in(pltpu.VMEM, query_all, cache_kv))

    received = lax.all_to_all(dense, "req", 0, 0, axis_index_groups=groups, tiled=True)

    partial_out = pl.pallas_call(
        merge,
        out_shape=pltpu.VMEM((heads,) + tile, f32),
        in_specs=vmem(4),
        out_specs=vmem(1)[0],
        compiler_params=params,
        name="merge",
    )(*held_in(pltpu.VMEM, received, own, recalled, w_out))

    half = heads // 2
    head_groups = [[(h + half) % heads for h in range(heads)]]
    terms = lax.all_to_all(partial_out, "head", 0, 0, axis_index_groups=head_groups, tiled=True)
    return jnp.sum(terms, axis=0)[:Q].astype(bf16)


def solution(mesh):
    in_specs = (
        P("req", None),
        P(),
        P(None, "head", None),
        P("head", None, None),
        P("req", "head", None, None),
        P("req", None, "head", None),
        P("req"),
        P("req"),
        P("head", None, None),
    )
    out_specs = P("req", "head")
    step = functools.partial(shards, 4, mesh.shape["req"] // 4)
    return jax.shard_map(step, mesh=mesh, in_specs=in_specs, out_specs=out_specs, check_vma=False)
```

```python
import functools

import jax
import jax.numpy as jnp
from jax import lax
from jax.experimental import pallas as pl
from jax.experimental.pallas import tpu as pltpu
from jax.sharding import PartitionSpec as P

DH = 128
NP = 16
Q = 5
ROWS = 8
PAIRS = 3
STRIDE = 16
PARTS = 3

masked_score = -1e30
norm_eps = 1e-06
kernel_vmem = 8 << 20
f32 = jnp.float32
bf16 = jnp.bfloat16


def iota(shape, axis):
    return lax.broadcasted_iota(jnp.int32, shape, axis)


def dot(a, b):
    return jnp.dot(a, b, preferred_element_type=f32)


def dot_t(a, b):
    return lax.dot_general(a, b, (((1,), (1,)), ((), ())), preferred_element_type=f32)


def stats_at(row, lane, offset):
    return (lane % STRIDE == row + offset) & (lane < PARTS * STRIDE)


def stats_row(peak, total, row, lane):
    picked = jnp.where(stats_at(row, lane, 0), peak, jnp.where(stats_at(row, lane, ROWS), total, 0.0))
    return jnp.sum(picked, axis=0, keepdims=True)


def stats_col(block, row, lane, offset):
    spread = jnp.broadcast_to(block[Q : Q + 1], row.shape)
    return jnp.sum(jnp.where(stats_at(row, lane, offset), spread, 0.0), axis=1, keepdims=True)


def packed(peak, total, summed, row, lane):
    stats = stats_row(peak, total, row, lane)
    high = stats.astype(bf16).astype(f32)
    rest = stats - high
    middle = rest.astype(bf16).astype(f32)
    place = lane[:1]
    tail = jnp.where(place < STRIDE, high, jnp.where(place < 2 * STRIDE, middle, rest - middle))
    return jnp.where(row < Q, summed, tail)


def put_block(target, index, tile):
    for k in range(PAIRS):
        target[index, k] = tile[2 * k : 2 * k + 2].astype(bf16)


def get_block(source, index):
    pairs = [source[index, k].astype(f32) for k in range(PAIRS)]
    return jnp.concatenate(pairs + [jnp.zeros((ROWS - 2 * PAIRS, DH), f32)], axis=0)


def project(tokens, gain, w_query, query_all, query, normed, padded):
    xf = tokens[...].astype(f32)
    inverse = lax.rsqrt(jnp.mean(xf * xf, axis=-1, keepdims=True) + norm_eps)
    normed[...] = (xf * inverse * gain[...]).astype(bf16)
    padded[...] = jnp.zeros_like(padded)
    padded[0:Q, :] = dot(normed[...], w_query[...])
    q = padded[...] * DH ** (-0.5)
    query[...] = q.astype(bf16)
    for k in range(PAIRS):
        pair = q[2 * k : 2 * k + 2].astype(bf16)
        query_all[:, k] = jnp.broadcast_to(pair[None], (query_all.shape[0],) + pair.shape)


def own_part(rows, columns, normed, query, w_key, w_value, persist_kv, memory, cache_kv, w_out, owner, length,
             own, recalled, cache_here, w_out_here, place, length_here, padded, owner_here, sems):
    pairs = ((owner, owner_here), (length, length_here), (cache_kv, cache_here), (w_out, w_out_here))
    copies = [pltpu.make_async_copy(a, b, sems.at[i]) for i, (a, b) in enumerate(pairs)]
    for copy in copies:
        copy.start()
    tile = (ROWS, DH)
    row, lane = iota(tile, 0), iota(tile, 1)
    padded[...] = jnp.zeros_like(padded)
    padded[0:Q, :DH] = dot(normed[...], w_key[...])
    padded[0:Q, DH:] = dot(normed[...], w_value[...])
    new_kv = padded[...].astype(bf16)
    q = query[...]
    score_persist = dot_t(q, persist_kv[:, :DH])
    score_new = dot_t(q, new_kv[:, :DH])
    causal = iota((ROWS, ROWS), 0) >= iota((ROWS, ROWS), 1)
    score_new = jnp.where(causal, score_new, masked_score)
    peak = jnp.maximum(
        jnp.max(score_persist, axis=-1, keepdims=True), jnp.max(score_new, axis=-1, keepdims=True)
    )
    weight_persist = jnp.exp(score_persist - peak)
    weight_new = jnp.exp(score_new - peak)
    total = jnp.sum(weight_persist, axis=-1, keepdims=True) + jnp.sum(weight_new, axis=-1, keepdims=True)
    summed = dot(weight_persist.astype(bf16), persist_kv[:, DH:])
    summed = summed + dot(weight_new.astype(bf16), new_kv[:, DH:])
    stats = stats_row(jnp.broadcast_to(peak, tile), jnp.broadcast_to(total, tile), row, lane)
    own[...] = jnp.where(row < Q, summed, jnp.where((row == Q) & (lane < STRIDE), stats, 0.0))
    recalled[...] = dot(q, memory[...])
    for copy in copies:
        copy.wait()
    for s in range(place.shape[0]):
        r = owner_here[s]
        x, z = lax.div(r, columns), lax.rem(r, columns)
        place[s] = lax.rem((z + columns // 2) * (columns // 2 + 1), columns) * rows + lax.rem((x + rows // 2) * (rows - 1), rows)


def attend(place, length, query_all, cache_kv, dense):
    pieces, slots = cache_kv.shape[0], cache_kv.shape[1]
    tile = (ROWS, DH)
    row, lane = iota(tile, 0), iota(tile, 1)

    for k in range(PAIRS):
        pair = (2, DH)
        holds_peak = (iota(pair, 0) + 2 * k == Q) & (iota(pair, 1) < ROWS)
        empty = jnp.where(holds_peak, masked_score, 0.0).astype(bf16)
        dense[:, k] = jnp.broadcast_to(empty[None], (dense.shape[0],) + pair)

    slot = iota((ROWS, slots), 1)
    scores = [
        dot_t(get_block(query_all, place[s]).astype(bf16), cache_kv[s, :, :DH]) for s in range(pieces)
    ]
    weights, peaks, totals = [], [], []
    for s in range(pieces):
        valid = slot < length[s]
        score = jnp.where(valid, scores[s], masked_score)
        peak = jnp.max(score, axis=-1, keepdims=True)
        weight = jnp.where(valid, jnp.exp(score - peak), 0.0)
        weights.append(weight.astype(bf16))
        peaks.append(jnp.broadcast_to(peak, tile))
        totals.append(jnp.broadcast_to(jnp.sum(weight, axis=-1, keepdims=True), tile))
    summeds = [dot(weights[s], cache_kv[s, :, DH:]) for s in range(pieces)]
    parts = list(zip(peaks, totals, summeds))

    for s in range(pieces):
        r = place[s]
        peaks = [jnp.where(jnp.full(tile, place[t], jnp.int32) == r, parts[t][0], 2 * masked_score) for t in range(pieces)]
        top = functools.reduce(jnp.maximum, peaks)
        scales = [jnp.exp(peak - top) for peak in peaks]
        total = sum(scale * part[1] for scale, part in zip(scales, parts))
        summed = sum(scale * part[2] for scale, part in zip(scales, parts))
        put_block(dense, r, packed(top, total, summed, row, lane))


def merge(received, own, recalled, w_out, partial_out):
    tile = (ROWS, DH)
    row, lane = iota(tile, 0), iota(tile, 1)
    sources = received.shape[0]
    blocks = [own[...]] + [get_block(received, s) for s in range(sources)]
    peaks = [stats_col(block, row, lane, 0) for block in blocks]
    peak = functools.reduce(jnp.maximum, peaks)
    summed = jnp.zeros(tile, f32)
    total = jnp.zeros((ROWS, 1), f32)
    for block, each in zip(blocks, peaks):
        scale = jnp.exp(each - peak)
        total = total + scale * stats_col(block, row, lane, ROWS)
        summed = summed + scale * block
    attended = summed / total
    head_out = jnp.where(row < Q, attended + recalled[...], 0.0).astype(bf16)
    terms = dot(head_out, w_out[...])
    for h in range(partial_out.shape[0]):
        to = (h + partial_out.shape[0] // 2) % partial_out.shape[0]
        partial_out[h] = terms[:, to * DH : (to + 1) * DH]


def held_in(space, *arrays):
    return [pltpu.with_memory_space_constraint(x, space) for x in arrays]


def vmem(n):
    return [pl.BlockSpec(memory_space=pltpu.VMEM)] * n


def smem(n):
    return [pl.BlockSpec(memory_space=pltpu.SMEM)] * n


def hbm(n):
    return [pl.BlockSpec(memory_space=pl.ANY)] * n


def column_block(d, j):
    return pl.BlockSpec((d, DH), lambda i: (0, j))


def exchange_order(rows, columns):
    return [
        (x * (rows - 1) + rows // 2) % rows * columns + (z * (columns // 2 + 1) + columns // 2) % columns
        for z in range(columns)
        for x in range(rows)
    ]


def shards(rows, columns, tokens, norm_gain, w_qkv, persist_kv, memory, cache_kv, piece_owner, piece_len, w_out):
    groups = [exchange_order(rows, columns)]
    heads = lax.axis_size("head")
    d = tokens.shape[1]
    pieces, slots = cache_kv.shape[:2]
    tile = (ROWS, DH)
    dense_shape = (rows * columns, PAIRS, 2, DH)
    params = pltpu.CompilerParams(vmem_limit_bytes=kernel_vmem)

    w_qkv, persist_kv, memory, cache_kv, w_out, piece_owner, piece_len = held_in(
        pltpu.HBM,
        w_qkv.reshape(d, 3 * DH),
        persist_kv.reshape(NP, 2 * DH),
        memory.reshape(DH, DH),
        cache_kv.reshape(pieces, slots, 2 * DH),
        w_out.reshape(DH, d),
        piece_owner,
        piece_len,
    )
    query_all, query, normed = pl.pallas_call(
        project,
        grid=(1,),
        out_shape=(pltpu.VMEM(dense_shape, bf16), pltpu.VMEM(tile, bf16), pltpu.VMEM(tokens.shape, bf16)),
        in_specs=vmem(2) + [column_block(d, 0)],
        out_specs=tuple(vmem(3)),
        scratch_shapes=[pltpu.VMEM(tile, f32)],
        compiler_params=params,
        name="project",
    )(*held_in(pltpu.HBM, tokens, norm_gain.reshape(1, d)), w_qkv)

    query_all = lax.all_to_all(query_all, "req", 0, 0, axis_index_groups=groups, tiled=True)

    own, recalled, cache_kv, w_out, place, piece_len = pl.pallas_call(
        functools.partial(own_part, rows, columns),
        grid=(1,),
        out_shape=(
            pltpu.VMEM(tile, f32),
            pltpu.VMEM(tile, f32),
            pltpu.VMEM(cache_kv.shape, bf16),
            pltpu.VMEM(w_out.shape, bf16),
            pltpu.SMEM((pieces,), jnp.int32),
            pltpu.SMEM((pieces,), jnp.int32),
        ),
        in_specs=vmem(2) + [column_block(d, 1), column_block(d, 2)] + vmem(2) + hbm(4),
        out_specs=tuple(vmem(4) + smem(2)),
        scratch_shapes=[
            pltpu.VMEM((ROWS, 2 * DH), f32),
            pltpu.SMEM((pieces,), jnp.int32),
            pltpu.SemaphoreType.DMA((4,)),
        ],
        compiler_params=params,
        name="own_part",
    )(*held_in(pltpu.VMEM, normed, query), w_qkv, w_qkv, persist_kv, memory, cache_kv, w_out, piece_owner, piece_len)

    dense = pl.pallas_call(
        attend,
        out_shape=pltpu.VMEM(dense_shape, bf16),
        in_specs=smem(2) + vmem(2),
        out_specs=vmem(1)[0],
        compiler_params=params,
        name="attend",
    )(*held_in(pltpu.SMEM, place, piece_len), *held_in(pltpu.VMEM, query_all, cache_kv))

    received = lax.all_to_all(dense, "req", 0, 0, axis_index_groups=groups, tiled=True)

    partial_out = pl.pallas_call(
        merge,
        out_shape=pltpu.VMEM((heads,) + tile, f32),
        in_specs=vmem(4),
        out_specs=vmem(1)[0],
        compiler_params=params,
        name="merge",
    )(*held_in(pltpu.VMEM, received, own, recalled, w_out))

    half = heads // 2
    head_groups = [[(h + half) % heads for h in range(heads)]]
    terms = lax.all_to_all(partial_out, "head", 0, 0, axis_index_groups=head_groups, tiled=True)
    return jnp.sum(terms, axis=0)[:Q].astype(bf16)


def solution(mesh):
    in_specs = (
        P("req", None),
        P(),
        P(None, "head", None),
        P("head", None, None),
        P("req", "head", None, None),
        P("req", None, "head", None),
        P("req"),
        P("req"),
        P("head", None, None),
    )
    out_specs = P("req", "head")
    step = functools.partial(shards, 4, mesh.shape["req"] // 4)
    return jax.shard_map(step, mesh=mesh, in_specs=in_specs, out_specs=out_specs, check_vma=False)
```
